32 devices in a mesh: tm: 8 (over z, x), rows: 4 (over y, core).
Axes of the slice: x: 2, y: 2, z: 4, core: 2. Of those that a mesh axis runs over, the one named last changes fastest.
Arguments:
- slc_stack: bfloat16 [32, 2, 32, 2048], P('tm', None, 'rows'), may hold values from -6 to 6
- partner_count: int32 [32], P('tm'), may hold values from 2 to 6, as said below
- look_sizes: int32 [32, 2], P('tm'), may hold values from 1 to 8, as said below
Outputs:
- interferogram: bfloat16 [32, 6, 2, 32, 2048], P('tm', None, None, 'rows')
- coherence: bfloat16 [32, 6, 32, 2048], P('tm', None, 'rows')
The draws below stay inside these ranges and needn't reach their ends.
Inputs may be any that keep to these rules, and one draw needn't show every extreme that they name: `partner_count`: some acquisition has 6 partners and some has 2. `look_sizes`: Half-heights run from 1 to 2, half-widths from 2 to 8; some acquisition has (2, 8) and some (1, 2).
All inputs are finite; a program needn't handle non-finite values.
Results may differ from the reference program's by a relative error of at most 0.0049.
Values may be sent and summed in bfloat16 or wider, within the bound.
A program may use at most 64 MiB of HBM per device.

```python
import jax
import jax.numpy as jnp
from jax import lax

MAXP = 6
HR = 2
HC = 8
COLS = 2048
ACQ = 32
IMG_ROWS = 32


def draw_partner_count(key, part):
    key_counts = jax.random.fold_in(key, 11)
    key_top = jax.random.fold_in(key, 12)
    key_low = jax.random.fold_in(key, 13)
    counts = jax.random.randint(key_counts, (ACQ,), 2, MAXP + 1)
    top_at = jax.random.randint(key_top, (), 0, ACQ)
    low_at = (top_at + 1 + jax.random.randint(key_low, (), 0, ACQ - 1)) % ACQ
    counts = counts.at[top_at].set(MAXP).at[low_at].set(2)
    return counts.astype(jnp.int32)


def draw_look_sizes(key, part):
    key_rows = jax.random.fold_in(key, 21)
    key_cols = jax.random.fold_in(key, 22)
    key_top = jax.random.fold_in(key, 23)
    key_low = jax.random.fold_in(key, 24)
    half_rows = jax.random.randint(key_rows, (ACQ,), 1, HR + 1)
    half_cols = jax.random.randint(key_cols, (ACQ,), 2, HC + 1)
    top_at = jax.random.randint(key_top, (), 0, ACQ)
    low_at = (top_at + 1 + jax.random.randint(key_low, (), 0, ACQ - 1)) % ACQ
    half_rows = half_rows.at[top_at].set(HR).at[low_at].set(1)
    half_cols = half_cols.at[top_at].set(HC).at[low_at].set(2)
    return jnp.stack([half_rows, half_cols], 1).astype(jnp.int32)


def levels(own_key, extent, split, least, top_value):
    loudness, own = 1.0, jax.random.fold_in(own_key, 6)
    for axis_at, blocks in split:
        heights = jnp.exp(jax.random.uniform(jax.random.fold_in(own, axis_at), (blocks,), jnp.float32, least / len(split), top_value / len(split)))
        loudness = loudness * jnp.repeat(heights, extent[axis_at] // blocks).reshape([-1 if axis == axis_at else 1 for axis in range(len(extent))])
    return loudness


def normal_values(stream_key, shape, width, reach, split=(), kind=jnp.bfloat16):
    array = width * jax.random.normal(stream_key, shape, jnp.float32)
    if split:
        array = array * levels(stream_key, shape, split, -0.22, 0.18)
    return jnp.clip(array, -reach, reach).astype(kind)


def setup_inputs(seed: int = 0) -> dict:
    key_of = jax.random.split(jax.random.key(seed), 4)
    return {
        "slc_stack": normal_values(key_of[0], (ACQ, 2, IMG_ROWS, COLS), 1.0, 6.0, ((0, 8), (2, 4))),
        "partner_count": draw_partner_count(jax.random.fold_in(key_of[3], 71), 0),
        "look_sizes": draw_look_sizes(jax.random.fold_in(key_of[3], 71), 0),
    }


epsilon = 1e-06

def window_rows(fields, half_rows):
    row_count = fields.shape[-2]
    padded = jnp.pad(fields, [(0, 0)] * (fields.ndim - 2) + [(HR, HR), (0, 0)])
    total = jnp.zeros(fields.shape, jnp.float32)
    for offset in range(-HR, HR + 1):
        piece = padded[..., HR + offset:HR + offset + row_count, :]
        total = total + jnp.where(abs(offset) <= half_rows, piece, 0.0)
    return total

def window_cols(summed, half_cols):
    col_count = summed.shape[-1]
    padded = jnp.pad(summed.astype(jnp.float32), [(0, 0)] * (summed.ndim - 1) + [(HC, HC)])
    total = jnp.zeros(summed.shape, jnp.float32)
    for offset in range(-HC, HC + 1):
        piece = padded[..., HC + offset:HC + offset + col_count]
        total = total + jnp.where(abs(offset) <= half_cols, piece, 0.0)
    return total

def reference(slc_stack, partner_count, look_sizes):
    acq_total = slc_stack.shape[0]

    def one_acquisition(acq_index):
        own = lax.dynamic_index_in_dim(slc_stack, acq_index, 0, keepdims=False).astype(jnp.float32)
        half_rows = look_sizes[acq_index, 0]
        half_cols = look_sizes[acq_index, 1]
        own_power = own[0] * own[0] + own[1] * own[1]
        boxed_own = window_cols(window_rows(own_power, half_rows).astype(jnp.bfloat16), half_cols)
        offsets = jnp.arange(1, MAXP + 1, dtype=jnp.int32)
        partner_index = jnp.minimum(acq_index + offsets, acq_total - 1).astype(jnp.int32)
        partners = slc_stack[partner_index].astype(jnp.float32)
        real_part = own[0] * partners[:, 0] + own[1] * partners[:, 1]
        imag_part = own[1] * partners[:, 0] - own[0] * partners[:, 1]
        power = partners[:, 0] * partners[:, 0] + partners[:, 1] * partners[:, 1]
        terms = jnp.stack([real_part, imag_part, power], 1)
        boxed = window_cols(window_rows(terms, half_rows).astype(jnp.bfloat16), half_cols)
        live = (offsets <= partner_count[acq_index]) & (acq_index + offsets < acq_total)
        area = ((2 * half_rows + 1) * (2 * half_cols + 1)).astype(jnp.float32)
        ifg = jnp.where(live[:, None, None, None], boxed[:, :2] / area, 0.0).astype(jnp.bfloat16)
        magnitude = jnp.sqrt(boxed[:, 0] * boxed[:, 0] + boxed[:, 1] * boxed[:, 1])
        coh = magnitude * lax.rsqrt(boxed_own[None] * boxed[:, 2] + epsilon)
        coh = jnp.where(live[:, None, None], coh, 0.0).astype(jnp.bfloat16)
        return (ifg, coh)
    interferogram, coherence = lax.map(one_acquisition, jnp.arange(acq_total, dtype=jnp.int32))
    return (interferogram, coherence)
```

```python
import functools
import itertools

import jax
import jax.numpy as jnp
from jax import lax
from jax.experimental import pallas as pl
from jax.experimental.pallas import tpu as pltpu
from jax.sharding import PartitionSpec as P

MAXP = 6
HR = 2
LANES = 128

epsilon = 1e-06
tiny = 1.2e-38
MESH = pl.DeviceIdType.MESH


class Pieces:
    def __init__(self, src, dst, send, recv, device):
        self.src, self.dst, self.send, self.recv, self.device = src, dst, send, recv, device

    def over(self, *at):
        return pltpu.make_async_remote_copy(
            src_ref=self.src.at[at] if at else self.src,
            dst_ref=self.dst.at[at] if at else self.dst,
            send_sem=self.send,
            recv_sem=self.recv,
            device_id=self.device,
            device_id_type=MESH,
        )

    def start(self):
        for at in itertools.product(*[range(size) for size in self.src.shape[:-2]]):
            self.over(*at).start()

    def wait_send(self):
        self.over().wait_send()

    def wait_recv(self):
        self.over().wait_recv()


def kernel(
    acq_total, counts_in, looks_in, x, ifg, coh,
    held, planes, power, sums_a, sums_b, lhs_a, lhs_b, bands, own_box, counts, looks,
    send_sem, recv_sem, local_sem, ready_sem,
):
    tm, line = lax.axis_index("tm"), lax.axis_index("rows")
    tm_count, line_count = lax.axis_size("tm"), lax.axis_size("rows")
    per_dev, _, rows, cols = x.shape
    total = held.shape[0]
    tiles = cols // LANES
    half = tiles // 2
    far = MAXP - per_dev
    ext_rows = rows + 2 * HR
    even = lax.rem(tm, 2) == 0
    odd = lax.rem(tm, 2) == 1
    below, above = line + 1 < line_count, line >= 1
    near_dev, far_dev, next_dev = {"tm": tm - 1}, {"tm": tm - 2}, {"tm": tm + 1}
    down_dev, up_dev = {"rows": line + 1}, {"rows": line - 1}

    local_copies = [
        pltpu.make_async_copy(x, held.at[pl.ds(0, per_dev), :, pl.ds(0, rows)], local_sem.at[0]),
        pltpu.make_async_copy(counts_in, counts, local_sem.at[1]),
        pltpu.make_async_copy(looks_in, looks, local_sem.at[2]),
    ]

    barrier = pltpu.get_barrier_semaphore()
    for there, device in [
        (tm + 1 < tm_count, next_dev),
        (tm + 2 < tm_count, {"tm": tm + 2}),
        (below, down_dev),
    ]:

        @pl.when(there)
        def _():
            pl.semaphore_signal(barrier, inc=1, device_id=device, device_id_type=MESH)

    earlier = sum(jnp.where(there, 1, 0) for there in (tm >= 1, tm >= 2, above))

    @pl.when(earlier > 0)
    def _():
        pl.semaphore_wait(barrier, earlier)

    for index, (there, device) in enumerate([(above, up_dev), (odd, near_dev)]):

        @pl.when(there)
        def _():
            pl.semaphore_signal(
                ready_sem.at[index], inc=1, device_id=device, device_id_type=MESH
            )

    starts = [per_dev, per_dev + far, 2 * per_dev]
    sizes = [far, per_dev - far, far]
    sides = [0, rows - HR]
    mid_slot = 6
    down_slot = mid_slot + MAXP
    up_slot = down_slot + 3
    own_slot = up_slot + 3
    onward_slot = own_slot + 2
    def copy(src, dst, send, recv, device):
        return Pieces(src, dst, send_sem.at[send], recv_sem.at[recv], device)

    def span(g, low, size):
        return held.at[pl.ds(starts[g], sizes[g]), :, pl.ds(low, size)]

    def edge(g, side, device):
        src = x.at[pl.ds(starts[g] % per_dev, sizes[g]), :, pl.ds(sides[side], HR)]
        return copy(src, span(g, sides[side], HR), 2 * g + side, 2 * g + side, device)

    def middle(p, device):
        src = x.at[p % per_dev, :, pl.ds(HR, rows - 2 * HR)]
        dst = held.at[p, :, pl.ds(HR, rows - 2 * HR)]
        at = mid_slot + p - per_dev
        return copy(src, dst, at, at, device)

    def onward_edge(side):
        low = sides[side]
        return copy(span(2, low, HR), span(0, low, HR), onward_slot + side, side, next_dev)

    def onward_middle(k):
        src = held.at[2 * per_dev + k, :, pl.ds(HR, rows - 2 * HR)]
        dst = held.at[per_dev + k, :, pl.ds(HR, rows - 2 * HR)]
        return copy(src, dst, onward_slot + 2 + k, mid_slot + k, next_dev)

    def down(g):
        return copy(span(g, rows - HR, HR), span(g, rows, HR), down_slot + g, down_slot + g, down_dev)

    def up(g):
        return copy(span(g, 0, HR), span(g, rows + HR, HR), up_slot + g, up_slot + g, up_dev)

    def own_down():
        src = x.at[:, :, pl.ds(rows - HR, HR)]
        dst = held.at[pl.ds(0, per_dev), :, pl.ds(rows, HR)]
        return copy(src, dst, own_slot, own_slot, down_dev)

    def own_up():
        src = x.at[:, :, pl.ds(0, HR)]
        dst = held.at[pl.ds(0, per_dev), :, pl.ds(rows + HR, HR)]
        return copy(src, dst, own_slot + 1, own_slot + 1, up_dev)

    has = [tm + 1 < tm_count, tm + 1 < tm_count, tm + 2 < tm_count]
    passes = even & has[2]
    sends = [odd, tm >= 1, tm >= 2]
    to = [near_dev, near_dev, far_dev]

    def when(condition, action):
        @pl.when(condition)
        def _():
            action()

    def send_edges(g):
        for side in range(2):
            edge(g, side, to[g]).start()

    def send_middles(g):
        for k in range(sizes[g]):
            middle(starts[g] + k, to[g]).start()

    when(above, lambda: own_up().start())
    for g in (2, 0, 1):
        when(sends[g], lambda: send_edges(g))
    for g in (2, 0, 1):
        when(sends[g], lambda: send_middles(g))
    for local_copy in local_copies:
        local_copy.start()

    def relay(g):
        def act():
            for side in range(2):
                edge(g, side, to[g]).wait_recv()
            when(below, lambda: down(g).start())
            when(above, lambda: up(g).start())

        when(has[g], act)

    def halo(g):
        when(has[g] & below, lambda: up(g).wait_recv())
        when(has[g] & above, lambda: down(g).wait_recv())

    def place(p, first, count, keep):
        for part in range(2):
            for t in range(tiles):
                lanes = slice(t * LANES, (t + 1) * LANES)
                v = held[p, part, first : first + count, lanes].astype(jnp.float32)
                if keep is not None:
                    v = jnp.where(keep, v, 0.0)
                planes[p, part, pl.ds(first * tiles + t, count, stride=tiles), :] = v

    order = [rows + k for k in range(HR)] + list(range(rows)) + [rows + HR + k for k in range(HR)]

    def plane(p, part, r, h):
        at = order[r] * tiles + h
        return planes[p, part, at : at + 8, :]

    side_row = lax.broadcasted_iota(jnp.int32, (2 * HR, LANES), 0)
    inside = ((side_row < HR) & above) | ((side_row >= HR) & below)
    near_edge = lax.broadcasted_iota(jnp.int32, (2 * rows, LANES), 1) < LANES // 2
    zero = jnp.zeros((rows, LANES), jnp.float32)

    def spread(get, count, out):
        pieces = [get(t) for t in range(-1, count + 1)]
        for t in range(0, count, 2):
            at = slice(t * rows, (t + 2) * rows)
            out[at, :LANES] = pieces[t + 1]
            out[at, LANES : 2 * LANES] = pieces[t + 2]
            out[at, 2 * LANES :] = jnp.where(near_edge, pieces[t + 3], pieces[t])

    def pair(first, second):
        return jnp.concatenate([first, second], 0).astype(jnp.bfloat16)

    def partner_power(p):
        for h in range(0, tiles, 8):
            v = []
            for r in range(ext_rows):
                re, im = plane(p, 0, r, h), plane(p, 1, r, h)
                v.append(re * re + im * im)
            pairs = [v[r] + v[r + 1] for r in range(1, rows + 2)]
            for r in range(rows):
                short = pairs[r] + v[r + 3]
                where = pl.ds(h * rows + r, 8, stride=rows)
                sums_a[0, where, :] = short
                sums_a[1, where, :] = short + (v[r] + v[r + 4])
        for n in range(2):

            def tile(t):
                return sums_a[n, t * rows : (t + 1) * rows, :] if 0 <= t < tiles else zero

            spread(lambda t: pair(tile(t), tile(t + half)), half, power.at[p, n])

    def boxed_power(a, p):
        result = jnp.dot(power[p, jnp.where(looks[0, a] >= HR, 1, 0)], bands[a], preferred_element_type=jnp.float32)
        result = result.reshape(half // 2, 2, rows, 2 * LANES)
        return [result[m % (half // 2), m // (half // 2)] for m in range(half)]

    def first_half(a, p, sums, lhs):
        outer = jnp.where(looks[0, a] >= HR, 1.0, 0.0).astype(jnp.float32)
        for h in range(0, tiles, 8):
            real, imag = [], []
            for r in range(ext_rows):
                own_re, own_im = plane(a, 0, r, h), plane(a, 1, r, h)
                far_re, far_im = plane(p, 0, r, h), plane(p, 1, r, h)
                real.append(own_re * far_re + own_im * far_im)
                imag.append(own_im * far_re - own_re * far_im)
            for field, v in enumerate((real, imag)):
                pairs = [v[r] + v[r + 1] for r in range(1, rows + 2)]
                for r in range(rows):
                    row_total = pairs[r] + v[r + 3] + (v[r] + v[r + 4]) * outer
                    sums[field, pl.ds(h * rows + r, 8, stride=rows), :] = row_total

        def fields(t):
            if not 0 <= t < tiles:
                return pair(zero, zero)
            return pair(*[sums[f, t * rows : (t + 1) * rows, :] for f in range(2)])

        spread(fields, tiles, lhs)

    def store(ref, at, value):
        for side in range(2):
            where = slice(at + side * LANES, at + (side + 1) * LANES)
            ref[:, where] = value[side * rows : (side + 1) * rows]

    def second_half(a, p, lhs):
        j = p - a - 1
        live = (j < counts[a]) & (tm * per_dev + p < acq_total)
        which = jnp.where(live, a, per_dev)
        boxed = jnp.dot(lhs[...], bands[which], preferred_element_type=jnp.float32)
        boxed = boxed.reshape(half, 2, rows, 2 * LANES)
        other = boxed_power(a, p)
        area = ((2 * looks[0, a] + 1) * (2 * looks[1, a] + 1)).astype(jnp.float32)
        scale = 1.0 / jnp.full((rows, 2 * LANES), area, jnp.float32)
        for m in range(half):
            re, im = boxed[m, 0], boxed[m, 1]
            size = re * re + im * im
            level = own_box[a, m] * other[m] + epsilon
            value = size * lax.rsqrt(jnp.maximum(size * level, tiny))
            for ref, v in ((ifg.at[a, j, 0], re * scale), (ifg.at[a, j, 1], im * scale), (coh.at[a, j], value)):
                store(ref, 2 * m * LANES, pair(v[:, :LANES], v[:, LANES:]))

    def slot(a, p, sums, lhs):
        first_half(a, p, sums, lhs)
        second_half(a, p, lhs)

    scratch = [(sums_a, lhs_a), (sums_b, lhs_b)]

    def slots(pairs):
        for n, (a, p) in enumerate(pairs):
            slot(a, p, *scratch[n % 2])

    for local_copy in local_copies:
        local_copy.wait()

    inner = lax.broadcasted_iota(jnp.int32, (3 * LANES, 2 * LANES), 0)
    across = lax.broadcasted_iota(jnp.int32, (3 * LANES, 2 * LANES), 1)
    source = jnp.where(inner < 2 * LANES + LANES // 2, inner, inner - 3 * LANES)
    distance = jnp.abs(source - across)
    bands[per_dev] = jnp.zeros((3 * LANES, 2 * LANES), jnp.bfloat16)

    @pl.loop(0, per_dev)
    def _(a):
        bands[a] = jnp.where(distance <= looks[1, a], 1.0, 0.0).astype(jnp.bfloat16)
        place(a, 0, rows, None)

    @pl.when(below)
    def _():
        pl.semaphore_wait(ready_sem.at[0], 1)
        own_down().start()

    @pl.when(even)
    def _():
        pl.semaphore_wait(ready_sem.at[1], 1)

    when(above, lambda: own_down().wait_recv())
    when(below, lambda: own_up().wait_recv())

    @pl.loop(0, per_dev)
    def _(a):
        place(a, rows, 2 * HR, inside)
        partner_power(a)
        box = boxed_power(a, a)
        for m in range(half):
            own_box[a, m] = box[m]

    own_pairs = [(a, p) for p in range(1, per_dev) for a in range(p)]
    early, late = own_pairs[: len(own_pairs) // 2], own_pairs[len(own_pairs) // 2 :]

    relay(2)

    @pl.when(passes)
    def _():
        for side in range(2):
            onward_edge(side).start()

    when(even, lambda: relay(0))
    slots(early)
    relay(1)
    slots(late)

    @pl.when(has[2])
    def _():
        for k in range(far):
            middle(2 * per_dev + k, far_dev).wait_recv()
            when(passes, lambda: onward_middle(k).start())

    when(odd, lambda: relay(0))

    def partner(p, there, first):
        place(p, 0, rows, there)
        place(p, rows, 2 * HR, inside & there)
        partner_power(p)
        slots([(a, p) for a in range(first, per_dev)])

    halo(2)
    for k in range(far):
        partner(2 * per_dev + k, has[2], 2 * per_dev + k - MAXP)

    def arrived(p):
        g = 0 if p < starts[1] else 1
        when(has[g], lambda: middle(p, to[g]).wait_recv())
        if p == starts[g]:
            halo(g)

    turns = list(range(starts[0], starts[2]))
    for p_even, p_odd in zip(turns, turns[far:] + turns[:far]):
        when(even, lambda: arrived(p_even))
        when(odd, lambda: arrived(p_odd))
        partner(jnp.where(odd, p_odd, p_even), has[0], 0)

    when(above, lambda: own_up().wait_send())
    when(below, lambda: own_down().wait_send())
    for g in range(3):
        when(has[g] & below, lambda: down(g).wait_send())
        when(has[g] & above, lambda: up(g).wait_send())

        @pl.when(sends[g])
        def _():
            for side in range(2):
                edge(g, side, to[g]).wait_send()
            for k in range(sizes[g]):
                middle(starts[g] + k, to[g]).wait_send()

    @pl.when(passes)
    def _():
        for side in range(2):
            onward_edge(side).wait_send()
        for k in range(far):
            onward_middle(k).wait_send()


def computed(x, counts, looks, acq_total):
    per_dev, parts, rows, cols = x.shape
    total, ext_rows = per_dev + MAXP, rows + 2 * HR
    tiles = cols // LANES
    slots = 16 + 2 * MAXP
    spare = max(0, 2 * per_dev - 1 - MAXP)
    hbm, vmem = [pl.BlockSpec(memory_space=space) for space in (pltpu.HBM, pltpu.VMEM)]
    return pl.pallas_call(
        functools.partial(kernel, acq_total),
        in_specs=[hbm, hbm, hbm],
        out_specs=[vmem, vmem],
        out_shape=[
            jax.ShapeDtypeStruct((per_dev, MAXP + spare, 2, rows, cols), jnp.bfloat16),
            jax.ShapeDtypeStruct((per_dev, MAXP + spare, rows, cols), jnp.bfloat16),
        ],
        scratch_shapes=[
            pltpu.VMEM((total, parts, 2 * rows, cols), x.dtype),
            pltpu.VMEM((total, parts, ext_rows * tiles, LANES), jnp.float32),
            pltpu.VMEM((total, 2, tiles // 2 * rows, 3 * LANES), jnp.bfloat16),
            pltpu.VMEM((2, tiles * rows, LANES), jnp.float32),
            pltpu.VMEM((2, tiles * rows, LANES), jnp.float32),
            pltpu.VMEM((tiles * rows, 3 * LANES), jnp.bfloat16),
            pltpu.VMEM((tiles * rows, 3 * LANES), jnp.bfloat16),
            pltpu.VMEM((per_dev + 1, 3 * LANES, 2 * LANES), jnp.bfloat16),
            pltpu.VMEM((per_dev, tiles // 2, rows, 2 * LANES), jnp.float32),
            pltpu.SMEM((per_dev,), jnp.int32),
            pltpu.SMEM((2, per_dev), jnp.int32),
            pltpu.SemaphoreType.DMA((slots,)),
            pltpu.SemaphoreType.DMA((slots,)),
            pltpu.SemaphoreType.DMA((3,)),
            pltpu.SemaphoreType.REGULAR((2,)),
        ],
        compiler_params=pltpu.CompilerParams(
            collective_id=0, has_side_effects=True, vmem_limit_bytes=40 * 1024 * 1024
        ),
        name="insar_boxes",
    )(*[pltpu.with_memory_space_constraint(operand, pltpu.HBM) for operand in (counts, looks, x)])


def write(ifg, coh, ifg_out, coh_out, sem):
    copies = []
    for a in range(ifg.shape[0]):
        for src, dst in ((ifg, ifg_out), (coh, coh_out)):
            kept = src.at[a, pl.ds(0, MAXP)]
            copies.append(pltpu.make_async_copy(kept, dst.at[a], sem.at[len(copies)]))
    for copy in copies:
        copy.start()
    for copy in copies:
        copy.wait()


def written(ifg, coh):
    shapes = [(v.shape[0], MAXP) + v.shape[2:] for v in (ifg, coh)]
    hbm, vmem = [pl.BlockSpec(memory_space=space) for space in (pltpu.HBM, pltpu.VMEM)]
    return pl.pallas_call(
        write,
        in_specs=[vmem, vmem],
        out_specs=[hbm, hbm],
        out_shape=[jax.ShapeDtypeStruct(shape, jnp.bfloat16) for shape in shapes],
        scratch_shapes=[pltpu.SemaphoreType.DMA((2 * ifg.shape[0],))],
        compiler_params=pltpu.CompilerParams(vmem_limit_bytes=2 * 1024 * 1024),
        name="insar_write",
    )(ifg, coh)


def local(slc_stack, partner_count, look_sizes):
    acq_total = lax.axis_size("tm") * slc_stack.shape[0]
    return tuple(written(*computed(slc_stack, partner_count, look_sizes.T, acq_total)))


def solution(mesh):
    return jax.shard_map(
        local,
        mesh=mesh,
        in_specs=(P("tm", None, "rows", None), P("tm"), P("tm", None)),
        out_specs=(P("tm", None, None, "rows", None), P("tm", None, "rows", None)),
        check_vma=False,
    )
```

```python
import functools
import itertools

import jax
import jax.numpy as jnp
from jax import lax
from jax.experimental import pallas as pl
from jax.experimental.pallas import tpu as pltpu
from jax.sharding import PartitionSpec as P

MAXP = 6
HR = 2
LANES = 128
LEAD = 8

epsilon = 1e-06
tiny = 1.2e-38
MESH = pl.DeviceIdType.MESH


class Pieces:
    def __init__(self, src, dst, send, recv, device):
        self.src, self.dst, self.send, self.recv, self.device = src, dst, send, recv, device

    def over(self, *at):
        return pltpu.make_async_remote_copy(
            src_ref=self.src.at[at] if at else self.src,
            dst_ref=self.dst.at[at] if at else self.dst,
            send_sem=self.send,
            recv_sem=self.recv,
            device_id=self.device,
            device_id_type=MESH,
        )

    def start(self):
        for at in itertools.product(*[range(size) for size in self.src.shape[:-2]]):
            self.over(*at).start()

    def wait_send(self):
        self.over().wait_send()

    def wait_recv(self):
        self.over().wait_recv()


def kernel(
    acq_total, counts_in, looks_in, x, ifg, coh,
    held, planes, power, power_sums, sums, lhs, bands, own_box, counts, looks,
    send_sem, recv_sem, local_sem, ready_sem,
):
    tm, line = lax.axis_index("tm"), lax.axis_index("rows")
    tm_count, line_count = lax.axis_size("tm"), lax.axis_size("rows")
    per_dev, _, rows, cols = x.shape
    total = held.shape[0]
    tiles = cols // LANES
    half = tiles // 2
    far = MAXP - per_dev
    ext_rows = rows + 2 * HR
    even = lax.rem(tm, 2) == 0
    odd = lax.rem(tm, 2) == 1
    below, above = line + 1 < line_count, line >= 1
    near_dev, far_dev, next_dev = {"tm": tm - 1}, {"tm": tm - 2}, {"tm": tm + 1}
    down_dev, up_dev = {"rows": line + 1}, {"rows": line - 1}

    local_copies = [
        pltpu.make_async_copy(x, held.at[pl.ds(0, per_dev), :, pl.ds(0, rows)], local_sem.at[0]),
        pltpu.make_async_copy(counts_in, counts, local_sem.at[1]),
        pltpu.make_async_copy(looks_in, looks, local_sem.at[2]),
    ]

    barrier = pltpu.get_barrier_semaphore()
    for there, device in [
        (even & (tm + 1 < tm_count), next_dev),
        (tm + 2 < tm_count, {"tm": tm + 2}),
        (below, down_dev),
    ]:

        @pl.when(there)
        def _():
            pl.semaphore_signal(barrier, inc=1, device_id=device, device_id_type=MESH)

    earlier = sum(jnp.where(there, 1, 0) for there in (odd, tm >= 2, above))

    @pl.when(earlier > 0)
    def _():
        pl.semaphore_wait(barrier, earlier)

    def tell(index, there, device):
        @pl.when(there)
        def _():
            pl.semaphore_signal(
                ready_sem.at[index], inc=1, device_id=device, device_id_type=MESH
            )

    def told(index, there):
        @pl.when(there)
        def _():
            pl.semaphore_wait(ready_sem.at[index], 1)

    tell(0, above, up_dev)
    tell(1, odd, near_dev)
    tell(2, even & (tm >= 2), far_dev)

    starts = [per_dev, per_dev + far, 2 * per_dev]
    sizes = [far, per_dev - far, far]
    sides = [0, rows - HR]
    mid_slot = 6
    down_slot = mid_slot + MAXP
    up_slot = down_slot + 3
    own_slot = up_slot + 3
    onward_slot = own_slot + 2
    def copy(src, dst, send, recv, device):
        return Pieces(src, dst, send_sem.at[send], recv_sem.at[recv], device)

    def span(g, low, size):
        return held.at[pl.ds(starts[g], sizes[g]), :, pl.ds(low, size)]

    def edge(g, side, device):
        src = x.at[pl.ds(starts[g] % per_dev, sizes[g]), :, pl.ds(sides[side], HR)]
        return copy(src, span(g, sides[side], HR), 2 * g + side, 2 * g + side, device)

    def middle(p, device):
        src = x.at[p % per_dev, :, pl.ds(HR, rows - 2 * HR)]
        dst = held.at[p, :, pl.ds(HR, rows - 2 * HR)]
        at = mid_slot + p - per_dev
        return copy(src, dst, at, at, device)

    def onward_edge(side):
        low = sides[side]
        return copy(span(2, low, HR), span(0, low, HR), onward_slot + side, side, next_dev)

    def onward_middle(k):
        src = held.at[2 * per_dev + k, :, pl.ds(HR, rows - 2 * HR)]
        dst = held.at[per_dev + k, :, pl.ds(HR, rows - 2 * HR)]
        return copy(src, dst, onward_slot + 2 + k, mid_slot + k, next_dev)

    def onward_halo(side):
        low = rows + side * HR
        recv = (down_slot, up_slot)[side]
        send = onward_slot + 2 + far + side
        return copy(span(2, low, HR), span(0, low, HR), send, recv, next_dev)

    def down(g):
        return copy(span(g, rows - HR, HR), span(g, rows, HR), down_slot + g, down_slot + g, down_dev)

    def up(g):
        return copy(span(g, 0, HR), span(g, rows + HR, HR), up_slot + g, up_slot + g, up_dev)

    def own_down():
        src = x.at[:, :, pl.ds(rows - HR, HR)]
        dst = held.at[pl.ds(0, per_dev), :, pl.ds(rows, HR)]
        return copy(src, dst, own_slot, own_slot, down_dev)

    def own_up():
        src = x.at[:, :, pl.ds(0, HR)]
        dst = held.at[pl.ds(0, per_dev), :, pl.ds(rows + HR, HR)]
        return copy(src, dst, own_slot + 1, own_slot + 1, up_dev)

    has = [tm + 1 < tm_count, tm + 1 < tm_count, tm + 2 < tm_count]
    passes = even & has[2]
    sends = [odd, tm >= 1, tm >= 2]
    to = [near_dev, near_dev, far_dev]

    line_even = lax.rem(line, 2) == 0
    far_down, far_up = below & ~line_even, above & line_even
    goes_down = [below & (even | line_even), below, below]
    goes_up = [above & (even | ~line_even), above, above]

    def when(condition, action):
        @pl.when(condition)
        def _():
            action()

    def send_edges(g):
        for side in range(2):
            edge(g, side, to[g]).start()

    def send_middles(g):
        for k in range(sizes[g]):
            middle(starts[g] + k, to[g]).start()

    when(above, lambda: own_up().start())
    when(sends[2], lambda: send_edges(2))
    when(sends[0], lambda: send_edges(0))
    when(odd, lambda: send_edges(1))
    for local_copy in local_copies:
        local_copy.start()

    def relay(g):
        def act():
            for side in range(2):
                edge(g, side, to[g]).wait_recv()
            when(goes_down[g], lambda: down(g).start())
            when(goes_up[g], lambda: up(g).start())

        when(has[g], act)

    def halo(g):
        when(has[g] & below, lambda: up(g).wait_recv())
        when(has[g] & above, lambda: down(g).wait_recv())

    def place(p, first, count, keep):
        for part in range(2):
            for t in range(tiles):
                lanes = slice(t * LANES, (t + 1) * LANES)
                v = held[p, part, first : first + count, lanes].astype(jnp.float32)
                if keep is not None:
                    v = jnp.where(keep, v, 0.0)
                planes[p, part, pl.ds(first * tiles + t, count, stride=tiles), :] = v

    order = [rows + k for k in range(HR)] + list(range(rows)) + [rows + HR + k for k in range(HR)]

    def plane(p, part, r, h):
        at = order[r] * tiles + h
        return planes[p, part, at : at + 8, :]

    side_row = lax.broadcasted_iota(jnp.int32, (2 * HR, LANES), 0)
    inside = ((side_row < HR) & above) | ((side_row >= HR) & below)
    near_edge = lax.broadcasted_iota(jnp.int32, (2 * rows, LANES), 1) < LANES // 2
    zero = jnp.zeros((rows, LANES), jnp.float32)

    def spread(get, count, out):
        pieces = [get(-1), get(0)]
        for t in range(0, count, 2):
            pieces += [get(t + 1), get(t + 2)]
            at = slice(t * rows, (t + 2) * rows)
            out[at, :LANES] = pieces[t + 1]
            out[at, LANES : 2 * LANES] = pieces[t + 2]
            out[at, 2 * LANES :] = jnp.where(near_edge, pieces[t + 3], pieces[t])
            yield

    def pair(first, second):
        return jnp.concatenate([first, second], 0).astype(jnp.bfloat16)

    def partner_power(p):
        for h in range(0, tiles, 8):
            v = []
            for r in range(ext_rows):
                re, im = plane(p, 0, r, h), plane(p, 1, r, h)
                v.append(re * re + im * im)
            pairs = [v[r] + v[r + 1] for r in range(1, rows + 2)]
            for r in range(rows):
                short = pairs[r] + v[r + 3]
                where = pl.ds(h * rows + r, 8, stride=rows)
                power_sums[0, where, :] = short
                power_sums[1, where, :] = short + (v[r] + v[r + 4])
        for n in range(2):

            def tile(t):
                return power_sums[n, t * rows : (t + 1) * rows, :] if 0 <= t < tiles else zero

            for _ in spread(lambda t: pair(tile(t), tile(t + half)), half, power.at[p, n]):
                pass

    def boxed_power(a, p):
        result = jnp.dot(power[p, jnp.where(looks[0, a] >= HR, 1, 0)], bands[a], preferred_element_type=jnp.float32)
        return paired(result)

    def paired(result):
        result = result.reshape(half // 2, 2, rows, 2 * LANES)
        return [result[m % (half // 2), m // (half // 2)] for m in range(half)]

    def first_half(a, p):
        middle_pair = [None, None]
        outer = jnp.where(looks[0, a] >= HR, 1.0, 0.0).astype(jnp.float32)
        for h in range(0, tiles, 8):
            real, imag = [], []
            for r in range(ext_rows):
                own_re, own_im = plane(a, 0, r, h), plane(a, 1, r, h)
                far_re, far_im = plane(p, 0, r, h), plane(p, 1, r, h)
                real.append(own_re * far_re + own_im * far_im)
                imag.append(own_im * far_re - own_re * far_im)
                if r < 2 * HR:
                    continue
                for field, v in enumerate((real, imag)):
                    first = r - 2 * HR
                    if first % 2 == 0:
                        middle_pair[field] = v[first + 2] + v[first + 3]
                        row_total = v[first + 1] + middle_pair[field]
                    else:
                        row_total = middle_pair[field] + v[first + 3]
                    row_total = row_total + (v[first] + v[first + 4]) * outer
                    sums[field, pl.ds(h * rows + first, 8, stride=rows), :] = row_total
                yield

        def fields(t):
            if not 0 <= t < tiles:
                return pair(zero, zero)
            return pair(*[sums[f, t * rows : (t + 1) * rows, :] for f in range(2)])

        yield from spread(fields, tiles, lhs)

    def store(ref, at, value):
        for side in range(2):
            where = slice(at + side * LANES, at + (side + 1) * LANES)
            ref[:, where] = value[side * rows : (side + 1) * rows]

    def second_half(a, p):
        j = p - a - 1
        live = (j < counts[a]) & (tm * per_dev + p < acq_total)
        shared = power[p, jnp.where(looks[0, a] >= HR, 1, 0)]
        stacked = jnp.concatenate([lhs[...], shared], 0)
        boxed = jnp.dot(stacked, bands[a], preferred_element_type=jnp.float32)
        other = paired(boxed[tiles * rows :])
        boxed = boxed[: tiles * rows].reshape(half, 2, rows, 2 * LANES)
        area = ((2 * looks[0, a] + 1) * (2 * looks[1, a] + 1)).astype(jnp.float32)
        alive = jnp.where(live, 1.0, 0.0).astype(jnp.float32)
        scale = alive / jnp.full((rows, 2 * LANES), area, jnp.float32)
        yield
        for m in range(half):
            re, im = boxed[m, 0], boxed[m, 1]
            size = re * re + im * im
            level = own_box[a, m] * other[m] + epsilon
            value = size * alive * lax.rsqrt(jnp.maximum(size * level, tiny))
            for ref, v in ((ifg.at[a, j, 0], re * scale), (ifg.at[a, j, 1], im * scale), (coh.at[a, j], value)):
                store(ref, 2 * m * LANES, pair(v[:, :LANES], v[:, LANES:]))
            yield

    opened = []

    def step(prologue, following):
        @pl.when(tm >= 0)
        def _():
            closing = second_half(*opened[0]) if opened else iter(())
            next(closing, None)
            prologue()
            opening = first_half(*following) if following else iter(())
            for _ in itertools.islice(opening, LEAD):
                pass
            for _ in closing:
                for _ in itertools.islice(opening, 2):
                    pass
            for _ in opening:
                pass

        opened[:] = [following] if following else []

    def slots(pairs, prologue=lambda: None):
        for n, following in enumerate(pairs):
            step(prologue if n == 0 else lambda: None, following)

    for local_copy in local_copies:
        local_copy.wait()

    inner = lax.broadcasted_iota(jnp.int32, (3 * LANES, 2 * LANES), 0)
    across = lax.broadcasted_iota(jnp.int32, (3 * LANES, 2 * LANES), 1)
    source = jnp.where(inner < 2 * LANES + LANES // 2, inner, inner - 3 * LANES)
    distance = jnp.abs(source - across)

    @pl.loop(0, per_dev)
    def _(a):
        bands[a] = jnp.where(distance <= looks[1, a], 1.0, 0.0).astype(jnp.bfloat16)
        place(a, 0, rows, None)

    told(0, below)
    when(below, lambda: own_down().start())
    told(1, even & (tm + 1 < tm_count))
    told(2, even & (tm + 2 < tm_count))
    tell(3, even & (tm + 2 < tm_count), {"tm": tm + 2})
    told(3, even & (tm >= 2))
    when(even & sends[1], lambda: send_edges(1))
    when(sends[2], lambda: send_middles(2))
    when(sends[0], lambda: send_middles(0))
    when(odd, lambda: send_middles(1))

    own_pairs = [(a, p) for p in range(1, per_dev) for a in range(p)]

    def own_halo():
        when(above, lambda: own_down().wait_recv())
        when(below, lambda: own_up().wait_recv())

    def own_work():
        @pl.loop(0, per_dev)
        def _(a):
            place(a, rows, 2 * HR, inside)
            partner_power(a)
            box = boxed_power(a, a)
            for m in range(half):
                own_box[a, m] = box[m]

        slots(own_pairs)
        step(lambda: None, None)

    outer_line = (line == 0) | (line == line_count - 1)

    @pl.when(outer_line)
    def _():
        own_halo()
        own_work()

    relay(2)

    @pl.when(passes)
    def _():
        for side in range(2):
            onward_edge(side).start()

    when(even, lambda: relay(0))
    when(~outer_line, own_halo)
    when(even & sends[1], lambda: send_middles(1))
    when(odd, lambda: relay(1))
    when(~outer_line, own_work)
    when(even, lambda: relay(1))

    @pl.when(has[2])
    def _():
        for k in range(far):
            middle(2 * per_dev + k, far_dev).wait_recv()
            when(passes, lambda: onward_middle(k).start())

    def partner(p, there, first):
        def prologue():
            place(p, 0, rows, there)
            place(p, rows, 2 * HR, inside & there)
            partner_power(p)

        slots([(a, p) for a in range(first, per_dev)], prologue)

    halo(2)
    when(passes & far_up, lambda: onward_halo(0).start())
    when(passes & far_down, lambda: onward_halo(1).start())
    for k in range(far):
        partner(2 * per_dev + k, has[2], 2 * per_dev + k - MAXP)
    when(odd, lambda: relay(0))

    def arrived(p):
        g = 0 if p < starts[1] else 1
        when(has[g], lambda: middle(p, to[g]).wait_recv())
        if p == starts[g]:
            halo(g)

    turns = list(range(starts[0], starts[2]))
    for p_even, p_odd in zip(turns, turns[far:] + turns[:far]):
        when(even, lambda: arrived(p_even))
        when(odd, lambda: arrived(p_odd))
        partner(jnp.where(odd, p_odd, p_even), has[0], 0)
    step(lambda: None, None)

    when(above, lambda: own_up().wait_send())
    when(below, lambda: own_down().wait_send())
    for g in range(3):
        when(has[g] & goes_down[g], lambda: down(g).wait_send())
        when(has[g] & goes_up[g], lambda: up(g).wait_send())

        @pl.when(sends[g])
        def _():
            for side in range(2):
                edge(g, side, to[g]).wait_send()
            for k in range(sizes[g]):
                middle(starts[g] + k, to[g]).wait_send()

    @pl.when(passes)
    def _():
        for side in range(2):
            onward_edge(side).wait_send()
        for k in range(far):
            onward_middle(k).wait_send()
        when(far_up, lambda: onward_halo(0).wait_send())
        when(far_down, lambda: onward_halo(1).wait_send())


def computed(x, counts, looks, acq_total):
    per_dev, parts, rows, cols = x.shape
    total, ext_rows = per_dev + MAXP, rows + 2 * HR
    tiles = cols // LANES
    slots = 16 + 2 * MAXP
    spare = max(0, 2 * per_dev - 1 - MAXP)
    hbm, vmem = [pl.BlockSpec(memory_space=space) for space in (pltpu.HBM, pltpu.VMEM)]
    return pl.pallas_call(
        functools.partial(kernel, acq_total),
        in_specs=[hbm, hbm, hbm],
        out_specs=[vmem, vmem],
        out_shape=[
            jax.ShapeDtypeStruct((per_dev, MAXP + spare, 2, rows, cols), jnp.bfloat16),
            jax.ShapeDtypeStruct((per_dev, MAXP + spare, rows, cols), jnp.bfloat16),
        ],
        scratch_shapes=[
            pltpu.VMEM((total, parts, 2 * rows, cols), x.dtype),
            pltpu.VMEM((total, parts, ext_rows * tiles, LANES), jnp.float32),
            pltpu.VMEM((total, 2, tiles // 2 * rows, 3 * LANES), jnp.bfloat16),
            pltpu.VMEM((2, tiles * rows, LANES), jnp.float32),
            pltpu.VMEM((2, tiles * rows, LANES), jnp.float32),
            pltpu.VMEM((tiles * rows, 3 * LANES), jnp.bfloat16),
            pltpu.VMEM((per_dev, 3 * LANES, 2 * LANES), jnp.bfloat16),
            pltpu.VMEM((per_dev, tiles // 2, rows, 2 * LANES), jnp.float32),
            pltpu.SMEM((per_dev,), jnp.int32),
            pltpu.SMEM((2, per_dev), jnp.int32),
            pltpu.SemaphoreType.DMA((slots,)),
            pltpu.SemaphoreType.DMA((slots,)),
            pltpu.SemaphoreType.DMA((3,)),
            pltpu.SemaphoreType.REGULAR((4,)),
        ],
        compiler_params=pltpu.CompilerParams(
            collective_id=0, has_side_effects=True, vmem_limit_bytes=40 * 1024 * 1024
        ),
        name="insar_boxes",
    )(*[pltpu.with_memory_space_constraint(operand, pltpu.HBM) for operand in (counts, looks, x)])


def write(ifg, coh, ifg_out, coh_out, sem):
    copies = []
    for a in range(ifg.shape[0]):
        for src, dst in ((ifg, ifg_out), (coh, coh_out)):
            kept = src.at[a, pl.ds(0, MAXP)]
            copies.append(pltpu.make_async_copy(kept, dst.at[a], sem.at[len(copies)]))
    for copy in copies:
        copy.start()
    for copy in copies:
        copy.wait()


def written(ifg, coh):
    shapes = [(v.shape[0], MAXP) + v.shape[2:] for v in (ifg, coh)]
    hbm, vmem = [pl.BlockSpec(memory_space=space) for space in (pltpu.HBM, pltpu.VMEM)]
    return pl.pallas_call(
        write,
        in_specs=[vmem, vmem],
        out_specs=[hbm, hbm],
        out_shape=[jax.ShapeDtypeStruct(shape, jnp.bfloat16) for shape in shapes],
        scratch_shapes=[pltpu.SemaphoreType.DMA((2 * ifg.shape[0],))],
        compiler_params=pltpu.CompilerParams(vmem_limit_bytes=2 * 1024 * 1024),
        name="insar_write",
    )(ifg, coh)


def local(slc_stack, partner_count, look_sizes):
    acq_total = lax.axis_size("tm") * slc_stack.shape[0]
    return tuple(written(*computed(slc_stack, partner_count, look_sizes.T, acq_total)))


def solution(mesh):
    return jax.shard_map(
        local,
        mesh=mesh,
        in_specs=(P("tm", None, "rows", None), P("tm"), P("tm", None)),
        out_specs=(P("tm", None, None, "rows", None), P("tm", None, "rows", None)),
        check_vma=False,
    )
```

```python
import functools
import itertools

import jax
import jax.numpy as jnp
from jax import lax
from jax.experimental import pallas as pl
from jax.experimental.pallas import tpu as pltpu
from jax.sharding import PartitionSpec as P

MAXP = 6
HR = 2
LANES = 128
LEAD = 8

epsilon = 1e-06
tiny = 1.2e-38
MESH = pl.DeviceIdType.MESH


class Pieces:
    def __init__(self, src, dst, send, recv, device):
        self.src, self.dst, self.send, self.recv, self.device = src, dst, send, recv, device

    def over(self, *at):
        return pltpu.make_async_remote_copy(
            src_ref=self.src.at[at] if at else self.src,
            dst_ref=self.dst.at[at] if at else self.dst,
            send_sem=self.send,
            recv_sem=self.recv,
            device_id=self.device,
            device_id_type=MESH,
        )

    def start(self):
        for at in itertools.product(*[range(size) for size in self.src.shape[:-2]]):
            self.over(*at).start()

    def wait_send(self):
        self.over().wait_send()

    def wait_recv(self):
        self.over().wait_recv()


def kernel(
    acq_total, counts_in, looks_in, x, ifg, coh,
    held, planes, power, power_sums, sums, lhs, bands, own_box, counts, looks,
    send_sem, recv_sem, local_sem, ready_sem,
):
    tm, line = lax.axis_index("tm"), lax.axis_index("rows")
    tm_count, line_count = lax.axis_size("tm"), lax.axis_size("rows")
    per_dev, _, rows, cols = x.shape
    total = held.shape[0]
    tiles = cols // LANES
    half = tiles // 2
    far = MAXP - per_dev
    ext_rows = rows + 2 * HR
    even = lax.rem(tm, 2) == 0
    odd = lax.rem(tm, 2) == 1
    below, above = line + 1 < line_count, line >= 1
    near_dev, far_dev, next_dev = {"tm": tm - 1}, {"tm": tm - 2}, {"tm": tm + 1}
    down_dev, up_dev = {"rows": line + 1}, {"rows": line - 1}

    local_copies = [
        pltpu.make_async_copy(x, held.at[pl.ds(0, per_dev), :, pl.ds(0, rows)], local_sem.at[0]),
        pltpu.make_async_copy(counts_in, counts, local_sem.at[1]),
        pltpu.make_async_copy(looks_in, looks, local_sem.at[2]),
    ]

    barrier = pltpu.get_barrier_semaphore()
    for there, device in [
        (even & (tm + 1 < tm_count), next_dev),
        (tm + 2 < tm_count, {"tm": tm + 2}),
        (below, down_dev),
    ]:

        @pl.when(there)
        def _():
            pl.semaphore_signal(barrier, inc=1, device_id=device, device_id_type=MESH)

    earlier = sum(jnp.where(there, 1, 0) for there in (odd, tm >= 2, above))

    @pl.when(earlier > 0)
    def _():
        pl.semaphore_wait(barrier, earlier)

    def tell(index, there, device):
        @pl.when(there)
        def _():
            pl.semaphore_signal(
                ready_sem.at[index], inc=1, device_id=device, device_id_type=MESH
            )

    def told(index, there):
        @pl.when(there)
        def _():
            pl.semaphore_wait(ready_sem.at[index], 1)

    tell(0, above, up_dev)
    tell(1, odd, near_dev)
    tell(2, even & (tm >= 2), far_dev)

    starts = [per_dev, per_dev + far, 2 * per_dev]
    sizes = [far, per_dev - far, far]
    sides = [0, rows - HR]
    mid_slot = 6
    down_slot = mid_slot + MAXP
    up_slot = down_slot + 3
    own_slot = up_slot + 3
    onward_slot = own_slot + 2
    def copy(src, dst, send, recv, device):
        return Pieces(src, dst, send_sem.at[send], recv_sem.at[recv], device)

    def span(g, low, size):
        return held.at[pl.ds(starts[g], sizes[g]), :, pl.ds(low, size)]

    def edge(g, side, device):
        src = x.at[pl.ds(starts[g] % per_dev, sizes[g]), :, pl.ds(sides[side], HR)]
        return copy(src, span(g, sides[side], HR), 2 * g + side, 2 * g + side, device)

    def middle(p, device):
        src = x.at[p % per_dev, :, pl.ds(HR, rows - 2 * HR)]
        dst = held.at[p, :, pl.ds(HR, rows - 2 * HR)]
        at = mid_slot + p - per_dev
        return copy(src, dst, at, at, device)

    def onward_edge(side):
        low = sides[side]
        return copy(span(2, low, HR), span(0, low, HR), onward_slot + side, side, next_dev)

    def onward_middle(k):
        src = held.at[2 * per_dev + k, :, pl.ds(HR, rows - 2 * HR)]
        dst = held.at[per_dev + k, :, pl.ds(HR, rows - 2 * HR)]
        return copy(src, dst, onward_slot + 2 + k, mid_slot + k, next_dev)

    def onward_halo(side):
        low = rows + side * HR
        recv = (down_slot, up_slot)[side]
        send = onward_slot + 2 + far + side
        return copy(span(2, low, HR), span(0, low, HR), send, recv, next_dev)

    def down(g):
        return copy(span(g, rows - HR, HR), span(g, rows, HR), down_slot + g, down_slot + g, down_dev)

    def up(g):
        return copy(span(g, 0, HR), span(g, rows + HR, HR), up_slot + g, up_slot + g, up_dev)

    def own_down():
        src = x.at[:, :, pl.ds(rows - HR, HR)]
        dst = held.at[pl.ds(0, per_dev), :, pl.ds(rows, HR)]
        return copy(src, dst, own_slot, own_slot, down_dev)

    def own_up():
        src = x.at[:, :, pl.ds(0, HR)]
        dst = held.at[pl.ds(0, per_dev), :, pl.ds(rows + HR, HR)]
        return copy(src, dst, own_slot + 1, own_slot + 1, up_dev)

    has = [tm + 1 < tm_count, tm + 1 < tm_count, tm + 2 < tm_count]
    passes = even & has[2]
    sends = [odd, tm >= 1, tm >= 2]
    to = [near_dev, near_dev, far_dev]

    line_even = lax.rem(line, 2) == 0
    far_down, far_up = below & ~line_even, above & line_even
    goes_down = [below & (even | line_even), below, below]
    goes_up = [above & (even | ~line_even), above, above]

    def when(condition, action):
        @pl.when(condition)
        def _():
            action()

    def send_edges(g):
        for side in range(2):
            edge(g, side, to[g]).start()

    def send_middles(g):
        for k in range(sizes[g]):
            middle(starts[g] + k, to[g]).start()

    when(above, lambda: own_up().start())
    when(sends[2], lambda: send_edges(2))
    when(sends[0], lambda: send_edges(0))
    when(odd, lambda: send_edges(1))
    for local_copy in local_copies:
        local_copy.start()

    def relay(g):
        def act():
            for side in range(2):
                edge(g, side, to[g]).wait_recv()
            when(goes_down[g], lambda: down(g).start())
            when(goes_up[g], lambda: up(g).start())

        when(has[g], act)

    def halo(g):
        when(has[g] & below, lambda: up(g).wait_recv())
        when(has[g] & above, lambda: down(g).wait_recv())

    def place(p, first, count, keep):
        for part in range(2):
            for t in range(tiles):
                lanes = slice(t * LANES, (t + 1) * LANES)
                v = held[p, part, first : first + count, lanes].astype(jnp.float32)
                if keep is not None:
                    v = jnp.where(keep, v, 0.0)
                planes[p, part, pl.ds(first * tiles + t, count, stride=tiles), :] = v

    order = [rows + k for k in range(HR)] + list(range(rows)) + [rows + HR + k for k in range(HR)]

    def plane(p, part, r, h):
        at = order[r] * tiles + h
        return planes[p, part, at : at + 8, :]

    side_row = lax.broadcasted_iota(jnp.int32, (2 * HR, LANES), 0)
    inside = ((side_row < HR) & above) | ((side_row >= HR) & below)
    near_edge = lax.broadcasted_iota(jnp.int32, (2 * rows, LANES), 1) < LANES // 2
    zero = jnp.zeros((rows, LANES), jnp.float32)

    def spread(get, count, out):
        pieces = [get(-1), get(0)]
        for t in range(0, count, 2):
            pieces += [get(t + 1), get(t + 2)]
            at = slice(t * rows, (t + 2) * rows)
            out[at, :LANES] = pieces[t + 1]
            out[at, LANES : 2 * LANES] = pieces[t + 2]
            out[at, 2 * LANES :] = jnp.where(near_edge, pieces[t + 3], pieces[t])
            yield

    def pair(first, second):
        return jnp.concatenate([first, second], 0).astype(jnp.bfloat16)

    def partner_power(p):
        for h in range(0, tiles, 8):
            v = []
            for r in range(ext_rows):
                re, im = plane(p, 0, r, h), plane(p, 1, r, h)
                v.append(re * re + im * im)
            pairs = [v[r] + v[r + 1] for r in range(1, rows + 2)]
            for r in range(rows):
                short = pairs[r] + v[r + 3]
                where = pl.ds(h * rows + r, 8, stride=rows)
                power_sums[0, where, :] = short
                power_sums[1, where, :] = short + (v[r] + v[r + 4])
        for n in range(2):

            def tile(t):
                return power_sums[n, t * rows : (t + 1) * rows, :] if 0 <= t < tiles else zero

            for _ in spread(lambda t: pair(tile(t), tile(t + half)), half, power.at[p, n]):
                pass

    def boxed_power(a, p):
        result = jnp.dot(power[p, jnp.where(looks[0, a] >= HR, 1, 0)], bands[a], preferred_element_type=jnp.float32)
        return paired(result)

    def paired(result):
        result = result.reshape(half // 2, 2, rows, 2 * LANES)
        return [result[m % (half // 2), m // (half // 2)] for m in range(half)]

    def first_half(a, p):
        middle_pair = [None, None]
        outer = jnp.where(looks[0, a] >= HR, 1.0, 0.0).astype(jnp.float32)
        for h in range(0, tiles, 8):
            real, imag = [], []
            for r in range(ext_rows):
                own_re, own_im = plane(a, 0, r, h), plane(a, 1, r, h)
                far_re, far_im = plane(p, 0, r, h), plane(p, 1, r, h)
                real.append(own_re * far_re + own_im * far_im)
                imag.append(own_im * far_re - own_re * far_im)
                if r < 2 * HR:
                    continue
                for field, v in enumerate((real, imag)):
                    first = r - 2 * HR
                    if first % 2 == 0:
                        middle_pair[field] = v[first + 2] + v[first + 3]
                        row_total = v[first + 1] + middle_pair[field]
                    else:
                        row_total = middle_pair[field] + v[first + 3]
                    row_total = row_total + (v[first] + v[first + 4]) * outer
                    sums[field, pl.ds(h * rows + first, 8, stride=rows), :] = row_total
                yield

        def fields(t):
            if not 0 <= t < tiles:
                return pair(zero, zero)
            return pair(*[sums[f, t * rows : (t + 1) * rows, :] for f in range(2)])

        yield from spread(fields, tiles, lhs)

    def store(ref, at, value):
        for side in range(2):
            where = slice(at + side * LANES, at + (side + 1) * LANES)
            ref[:, where] = value[side * rows : (side + 1) * rows]

    def second_half(a, p):
        j = p - a - 1
        live = (j < counts[a]) & (tm * per_dev + p < acq_total)
        shared = power[p, jnp.where(looks[0, a] >= HR, 1, 0)]
        stacked = jnp.concatenate([lhs[...], shared], 0)
        boxed = jnp.dot(stacked, bands[a], preferred_element_type=jnp.float32)
        other = paired(boxed[tiles * rows :])
        boxed = boxed[: tiles * rows].reshape(half, 2, rows, 2 * LANES)
        area = ((2 * looks[0, a] + 1) * (2 * looks[1, a] + 1)).astype(jnp.float32)
        alive = jnp.where(live, 1.0, 0.0).astype(jnp.float32)
        scale = alive / jnp.full((rows, 2 * LANES), area, jnp.float32)
        yield
        for m in range(half):
            re, im = boxed[m, 0], boxed[m, 1]
            size = re * re + im * im
            level = own_box[a, m] * other[m] + epsilon
            value = size * alive * lax.rsqrt(jnp.maximum(size * level, tiny))
            for ref, v in ((ifg.at[a, j, 0], re * scale), (ifg.at[a, j, 1], im * scale), (coh.at[a, j], value)):
                store(ref, 2 * m * LANES, pair(v[:, :LANES], v[:, LANES:]))
            yield

    opened = []

    def step(prologue, following):
        @pl.when(tm >= 0)
        def _():
            closing = second_half(*opened[0]) if opened else iter(())
            next(closing, None)
            prologue()
            opening = first_half(*following) if following else iter(())
            for _ in itertools.islice(opening, LEAD):
                pass
            for _ in closing:
                for _ in itertools.islice(opening, 2):
                    pass
            for _ in opening:
                pass

        opened[:] = [following] if following else []

    def slots(pairs, prologue=lambda: None):
        for n, following in enumerate(pairs):
            step(prologue if n == 0 else lambda: None, following)

    for local_copy in local_copies:
        local_copy.wait()

    inner = lax.broadcasted_iota(jnp.int32, (3 * LANES, 2 * LANES), 0)
    across = lax.broadcasted_iota(jnp.int32, (3 * LANES, 2 * LANES), 1)
    source = jnp.where(inner < 2 * LANES + LANES // 2, inner, inner - 3 * LANES)
    distance = jnp.abs(source - across)

    @pl.loop(0, per_dev)
    def _(a):
        bands[a] = jnp.where(distance <= looks[1, a], 1.0, 0.0).astype(jnp.bfloat16)
        place(a, 0, rows, None)

    told(0, below)
    when(below, lambda: own_down().start())
    told(1, even & (tm + 1 < tm_count))
    told(2, even & (tm + 2 < tm_count))
    tell(3, even & (tm + 2 < tm_count), {"tm": tm + 2})
    told(3, even & (tm >= 2))
    when(even & sends[1], lambda: send_edges(1))
    when(sends[2], lambda: send_middles(2))
    when(sends[0], lambda: send_middles(0))
    when(odd, lambda: send_middles(1))

    own_pairs = [(a, p) for p in range(1, per_dev) for a in range(p)]

    def own_halo():
        when(above, lambda: own_down().wait_recv())
        when(below, lambda: own_up().wait_recv())

    def own_work():
        @pl.loop(0, per_dev)
        def _(a):
            place(a, rows, 2 * HR, inside)
            partner_power(a)
            box = boxed_power(a, a)
            for m in range(half):
                own_box[a, m] = box[m]

        slots(own_pairs)
        step(lambda: None, None)

    outer_line = (line == 0) | (line == line_count - 1)

    @pl.when(outer_line)
    def _():
        own_halo()
        own_work()

    relay(2)

    @pl.when(passes)
    def _():
        for side in range(2):
            onward_edge(side).start()

    when(even, lambda: relay(0))
    when(~outer_line, own_halo)
    when(even & sends[1], lambda: send_middles(1))
    when(odd, lambda: relay(1))
    when(~outer_line, own_work)
    when(even, lambda: relay(1))

    @pl.when(has[2])
    def _():
        for k in range(far):
            middle(2 * per_dev + k, far_dev).wait_recv()
            when(passes, lambda: onward_middle(k).start())

    def partners(chosen, there, placed=False):
        def prologue():
            for p, _ in chosen:
                if not placed:
                    place(p, 0, rows, there)
                place(p, rows, 2 * HR, inside & there)
            for p, _ in chosen:
                partner_power(p)

        slots([(a, p) for p, first in chosen for a in range(first, per_dev)], prologue)

    ends = [2 * per_dev + k for k in range(far)]
    for p in ends:
        place(p, 0, rows, has[2])
    halo(2)
    when(passes & far_up, lambda: onward_halo(0).start())
    when(passes & far_down, lambda: onward_halo(1).start())
    partners([(p, p - MAXP) for p in ends], has[2], placed=True)
    when(odd, lambda: relay(0))

    def arrived(p):
        g = 0 if p < starts[1] else 1
        when(has[g], lambda: middle(p, to[g]).wait_recv())
        if p == starts[g]:
            halo(g)

    def arrive(group):
        for p in group:
            arrived(p)

    turns = list(range(starts[0], starts[2]))
    swapped = turns[far:] + turns[:far]
    for n in range(0, per_dev, 2):
        when(even, lambda: arrive(turns[n : n + 2]))
        when(odd, lambda: arrive(swapped[n : n + 2]))
        both = zip(turns[n : n + 2], swapped[n : n + 2])
        partners([(jnp.where(odd, p_odd, p_even), 0) for p_even, p_odd in both], has[0])
    step(lambda: None, None)

    when(above, lambda: own_up().wait_send())
    when(below, lambda: own_down().wait_send())
    for g in range(3):
        when(has[g] & goes_down[g], lambda: down(g).wait_send())
        when(has[g] & goes_up[g], lambda: up(g).wait_send())

        @pl.when(sends[g])
        def _():
            for side in range(2):
                edge(g, side, to[g]).wait_send()
            for k in range(sizes[g]):
                middle(starts[g] + k, to[g]).wait_send()

    @pl.when(passes)
    def _():
        for side in range(2):
            onward_edge(side).wait_send()
        for k in range(far):
            onward_middle(k).wait_send()
        when(far_up, lambda: onward_halo(0).wait_send())
        when(far_down, lambda: onward_halo(1).wait_send())


def computed(x, counts, looks, acq_total):
    per_dev, parts, rows, cols = x.shape
    total, ext_rows = per_dev + MAXP, rows + 2 * HR
    tiles = cols // LANES
    slots = 16 + 2 * MAXP
    spare = max(0, 2 * per_dev - 1 - MAXP)
    hbm, vmem = [pl.BlockSpec(memory_space=space) for space in (pltpu.HBM, pltpu.VMEM)]
    return pl.pallas_call(
        functools.partial(kernel, acq_total),
        in_specs=[hbm, hbm, hbm],
        out_specs=[vmem, vmem],
        out_shape=[
            jax.ShapeDtypeStruct((per_dev, MAXP + spare, 2, rows, cols), jnp.bfloat16),
            jax.ShapeDtypeStruct((per_dev, MAXP + spare, rows, cols), jnp.bfloat16),
        ],
        scratch_shapes=[
            pltpu.VMEM((total, parts, 2 * rows, cols), x.dtype),
            pltpu.VMEM((total, parts, ext_rows * tiles, LANES), jnp.float32),
            pltpu.VMEM((total, 2, tiles // 2 * rows, 3 * LANES), jnp.bfloat16),
            pltpu.VMEM((2, tiles * rows, LANES), jnp.float32),
            pltpu.VMEM((2, tiles * rows, LANES), jnp.float32),
            pltpu.VMEM((tiles * rows, 3 * LANES), jnp.bfloat16),
            pltpu.VMEM((per_dev, 3 * LANES, 2 * LANES), jnp.bfloat16),
            pltpu.VMEM((per_dev, tiles // 2, rows, 2 * LANES), jnp.float32),
            pltpu.SMEM((per_dev,), jnp.int32),
            pltpu.SMEM((2, per_dev), jnp.int32),
            pltpu.SemaphoreType.DMA((slots,)),
            pltpu.SemaphoreType.DMA((slots,)),
            pltpu.SemaphoreType.DMA((3,)),
            pltpu.SemaphoreType.REGULAR((4,)),
        ],
        compiler_params=pltpu.CompilerParams(
            collective_id=0, has_side_effects=True, vmem_limit_bytes=40 * 1024 * 1024
        ),
        name="insar_boxes",
    )(*[pltpu.with_memory_space_constraint(operand, pltpu.HBM) for operand in (counts, looks, x)])


def write(ifg, coh, ifg_out, coh_out, sem):
    copies = []
    for a in range(ifg.shape[0]):
        for src, dst in ((ifg, ifg_out), (coh, coh_out)):
            kept = src.at[a, pl.ds(0, MAXP)]
            copies.append(pltpu.make_async_copy(kept, dst.at[a], sem.at[len(copies)]))
    for copy in copies:
        copy.start()
    for copy in copies:
        copy.wait()


def written(ifg, coh):
    shapes = [(v.shape[0], MAXP) + v.shape[2:] for v in (ifg, coh)]
    hbm, vmem = [pl.BlockSpec(memory_space=space) for space in (pltpu.HBM, pltpu.VMEM)]
    return pl.pallas_call(
        write,
        in_specs=[vmem, vmem],
        out_specs=[hbm, hbm],
        out_shape=[jax.ShapeDtypeStruct(shape, jnp.bfloat16) for shape in shapes],
        scratch_shapes=[pltpu.SemaphoreType.DMA((2 * ifg.shape[0],))],
        compiler_params=pltpu.CompilerParams(vmem_limit_bytes=2 * 1024 * 1024),
        name="insar_write",
    )(ifg, coh)


def local(slc_stack, partner_count, look_sizes):
    acq_total = lax.axis_size("tm") * slc_stack.shape[0]
    return tuple(written(*computed(slc_stack, partner_count, look_sizes.T, acq_total)))


def solution(mesh):
    return jax.shard_map(
        local,
        mesh=mesh,
        in_specs=(P("tm", None, "rows", None), P("tm"), P("tm", None)),
        out_specs=(P("tm", None, None, "rows", None), P("tm", None, "rows", None)),
        check_vma=False,
    )
```

```python
import functools
import itertools

import jax
import jax.numpy as jnp
from jax import lax
from jax.experimental import pallas as pl
from jax.experimental.pallas import tpu as pltpu
from jax.sharding import PartitionSpec as P

MAXP = 6
HR = 2
LANES = 128
LEAD = 8

epsilon = 1e-06
tiny = 1.2e-38
MESH = pl.DeviceIdType.MESH


class Pieces:
    def __init__(self, src, dst, send, recv, device):
        self.src, self.dst, self.send, self.recv, self.device = src, dst, send, recv, device

    def over(self, *at):
        return pltpu.make_async_remote_copy(
            src_ref=self.src.at[at] if at else self.src,
            dst_ref=self.dst.at[at] if at else self.dst,
            send_sem=self.send,
            recv_sem=self.recv,
            device_id=self.device,
            device_id_type=MESH,
        )

    def start(self):
        for at in itertools.product(*[range(size) for size in self.src.shape[:-2]]):
            self.over(*at).start()

    def wait_send(self):
        self.over().wait_send()

    def wait_recv(self):
        self.over().wait_recv()


class Slots:
    def __init__(
        self, tm, line, acq_total, dims, planes, power_sums, sums, lhs, bands, own_box, counts, looks
    ):
        self.tm, self.acq_total, self.dims = tm, acq_total, dims
        self.planes, self.power_sums, self.sums, self.lhs = planes, power_sums, sums, lhs
        self.bands, self.own_box, self.counts, self.looks = bands, own_box, counts, looks
        rows = dims[1]
        self.tiles = dims[2] // LANES
        side_row = lax.broadcasted_iota(jnp.int32, (2 * HR, LANES), 0)
        above, below = line >= 1, line + 1 < lax.axis_size("rows")
        self.inside = ((side_row < HR) & above) | ((side_row >= HR) & below)
        self.near_edge = lax.broadcasted_iota(jnp.int32, (2 * rows, LANES), 1) < LANES // 2
        self.zero = jnp.zeros((rows, LANES), jnp.float32)
        self.order = [rows + k for k in range(HR)] + list(range(rows))
        self.order += [rows + HR + k for k in range(HR)]
        self.opened = []

    def place(self, src, dst, first, count, keep):
        for part in range(2):
            for t in range(self.tiles):
                v = src[part, first : first + count, t * LANES : (t + 1) * LANES]
                v = v.astype(jnp.float32)
                if keep is not None:
                    v = jnp.where(keep, v, 0.0)
                dst[part, pl.ds(first * self.tiles + t, count, stride=self.tiles), :] = v

    def plane(self, ref, part, r, h):
        at = self.order[r] * self.tiles + h
        return ref[part, at : at + 8, :]

    def spread(self, get, count, out):
        rows = self.dims[1]
        pieces = [get(-1), get(0)]
        for t in range(0, count, 2):
            pieces += [get(t + 1), get(t + 2)]
            at = slice(t * rows, (t + 2) * rows)
            out[at, :LANES] = pieces[t + 1]
            out[at, LANES : 2 * LANES] = pieces[t + 2]
            out[at, 2 * LANES :] = jnp.where(self.near_edge, pieces[t + 3], pieces[t])
            yield

    def partner_power(self, ref, out):
        rows, tiles = self.dims[1], self.tiles
        half = tiles // 2
        for h in range(0, tiles, 8):
            v = []
            for r in range(rows + 2 * HR):
                re, im = self.plane(ref, 0, r, h), self.plane(ref, 1, r, h)
                v.append(re * re + im * im)
            pairs = [v[r] + v[r + 1] for r in range(1, rows + 2)]
            for r in range(rows):
                short = pairs[r] + v[r + 3]
                where = pl.ds(h * rows + r, 8, stride=rows)
                self.power_sums[0, where, :] = short
                self.power_sums[1, where, :] = short + (v[r] + v[r + 4])
        for n in range(2):

            def tile(t):
                inside = 0 <= t < tiles
                return self.power_sums[n, t * rows : (t + 1) * rows, :] if inside else self.zero

            for _ in self.spread(lambda t: pair(tile(t), tile(t + half)), half, out.at[n]):
                pass

    def outer(self, a):
        return jnp.where(self.looks[0, a] >= HR, 1.0, 0.0).astype(jnp.float32)

    def factors(self, a, p):
        per_dev, rows, _ = self.dims
        live = (p - a - 1 < self.counts[a]) & (self.tm * per_dev + p < self.acq_total)
        area = ((2 * self.looks[0, a] + 1) * (2 * self.looks[1, a] + 1)).astype(jnp.float32)
        alive = jnp.where(live, 1.0, 0.0).astype(jnp.float32)
        return alive, alive / jnp.full((rows, LANES), area, jnp.float32)

    def chosen(self, a, power):
        return power[jnp.where(self.looks[0, a] >= HR, 1, 0)]

    def paired(self, result):
        quarter = self.tiles // 4
        result = result.reshape(quarter, 2, self.dims[1], 2 * LANES)
        return [result[m % quarter, m // quarter] for m in range(2 * quarter)]

    def boxed_power(self, a, power):
        result = jnp.dot(
            self.chosen(a, power), self.bands[a], preferred_element_type=jnp.float32
        )
        return self.paired(result)

    def first_half(self, a, far):
        rows, tiles, own = self.dims[1], self.tiles, self.planes.at[a]
        middle_pair = [None, None]
        outer = self.outer(a)
        for h in range(0, tiles, 8):
            real, imag = [], []
            for r in range(rows + 2 * HR):
                own_re, own_im = self.plane(own, 0, r, h), self.plane(own, 1, r, h)
                far_re, far_im = self.plane(far, 0, r, h), self.plane(far, 1, r, h)
                real.append(own_re * far_re + own_im * far_im)
                imag.append(own_im * far_re - own_re * far_im)
                if r < 2 * HR:
                    continue
                for field, v in enumerate((real, imag)):
                    first = r - 2 * HR
                    if first % 2 == 0:
                        middle_pair[field] = v[first + 2] + v[first + 3]
                        row_total = v[first + 1] + middle_pair[field]
                    else:
                        row_total = middle_pair[field] + v[first + 3]
                    row_total = row_total + (v[first] + v[first + 4]) * outer
                    self.sums[field, pl.ds(h * rows + first, 8, stride=rows), :] = row_total
                yield

        def fields(t):
            if not 0 <= t < tiles:
                return pair(self.zero, self.zero)
            return pair(*[self.sums[f, t * rows : (t + 1) * rows, :] for f in range(2)])

        yield from self.spread(fields, tiles, self.lhs)

    def store(self, ref, at, value):
        rows = self.dims[1]
        for side in range(2):
            where = slice(at + side * LANES, at + (side + 1) * LANES)
            ref[:, where] = value[side * rows : (side + 1) * rows]

    def second_half(self, a, p, power, ifg, coh):
        rows, half = self.dims[1], self.tiles // 2
        stacked = jnp.concatenate([self.lhs[...], self.chosen(a, power)], 0)
        boxed = jnp.dot(stacked, self.bands[a], preferred_element_type=jnp.float32)
        other = self.paired(boxed[self.tiles * rows :])
        boxed = boxed[: self.tiles * rows].reshape(half, 2, rows, 2 * LANES)
        alive, scale = self.factors(a, p)
        scale = jnp.concatenate([scale, scale], 1)
        if alive.ndim:
            alive = jnp.concatenate([alive, alive], 1)
        yield
        for m in range(half):
            re, im = boxed[m, 0], boxed[m, 1]
            size = re * re + im * im
            level = self.own_box[a, m] * other[m] + epsilon
            value = size * alive * lax.rsqrt(jnp.maximum(size * level, tiny))
            for ref, v in ((ifg.at[0], re * scale), (ifg.at[1], im * scale), (coh, value)):
                self.store(ref, 2 * m * LANES, pair(v[:, :LANES], v[:, LANES:]))
            yield

    def step(self, following, prologue=lambda: None):
        closing = iter(())
        if self.opened:
            a, p, _, power, ifg, coh = self.opened.pop()
            closing = self.second_half(a, p, power, ifg, coh)
        next(closing, None)
        prologue()
        opening = iter(())
        if following is not None:
            opening = self.first_half(following[0], following[2])
            self.opened.append(following)
        for _ in itertools.islice(opening, LEAD):
            pass
        for _ in closing:
            for _ in itertools.islice(opening, 2):
                pass
        for _ in opening:
            pass

    def slots(self, lanes, prologue=lambda: None):
        for n, following in enumerate(lanes):
            self.step(following, prologue if n == 0 else lambda: None)


class LateSlots(Slots):
    def outer(self, a):
        return self.counts[a, 0]

    def factors(self, a, k):
        return self.counts[a, 1 + k], self.counts[a, 3 + k]

    def chosen(self, a, power):
        wide = self.outer(a)[:1] > 0.5
        wide = jnp.broadcast_to(jnp.concatenate([wide] * 3, 1), power.shape[1:])
        return jnp.where(wide, power[1], power[0])


def pair(first, second):
    return jnp.concatenate([first, second], 0).astype(jnp.bfloat16)


def kernel(
    acq_total, counts_in, looks_in, x, ifg, coh, held, planes, bands, own_box, factors,
    power, power_sums, sums, lhs, counts, looks,
    send_sem, recv_sem, local_sem, ready_sem,
):
    tm, line = lax.axis_index("tm"), lax.axis_index("rows")
    tm_count, line_count = lax.axis_size("tm"), lax.axis_size("rows")
    per_dev, _, rows, cols = x.shape
    total = held.shape[0]
    tiles = cols // LANES
    half = tiles // 2
    far = MAXP - per_dev
    ext_rows = rows + 2 * HR
    even = lax.rem(tm, 2) == 0
    odd = lax.rem(tm, 2) == 1
    below, above = line + 1 < line_count, line >= 1
    near_dev, far_dev, next_dev = {"tm": tm - 1}, {"tm": tm - 2}, {"tm": tm + 1}
    down_dev, up_dev = {"rows": line + 1}, {"rows": line - 1}

    local_copies = [
        pltpu.make_async_copy(x, held.at[pl.ds(0, per_dev), :, pl.ds(0, rows)], local_sem.at[0]),
        pltpu.make_async_copy(counts_in, counts, local_sem.at[1]),
        pltpu.make_async_copy(looks_in, looks, local_sem.at[2]),
    ]

    barrier = pltpu.get_barrier_semaphore()
    for there, device in [
        (even & (tm + 1 < tm_count), next_dev),
        (tm + 2 < tm_count, {"tm": tm + 2}),
        (below, down_dev),
    ]:

        @pl.when(there)
        def _():
            pl.semaphore_signal(barrier, inc=1, device_id=device, device_id_type=MESH)

    earlier = sum(jnp.where(there, 1, 0) for there in (odd, tm >= 2, above))

    @pl.when(earlier > 0)
    def _():
        pl.semaphore_wait(barrier, earlier)

    def tell(index, there, device):
        @pl.when(there)
        def _():
            pl.semaphore_signal(
                ready_sem.at[index], inc=1, device_id=device, device_id_type=MESH
            )

    def told(index, there):
        @pl.when(there)
        def _():
            pl.semaphore_wait(ready_sem.at[index], 1)

    tell(0, above, up_dev)
    tell(1, odd, near_dev)
    tell(2, even & (tm >= 2), far_dev)

    starts = [per_dev, per_dev + far, 2 * per_dev]
    sizes = [far, per_dev - far, far]
    sides = [0, rows - HR]
    mid_slot = 6
    down_slot = mid_slot + MAXP
    up_slot = down_slot + 3
    own_slot = up_slot + 3
    onward_slot = own_slot + 2
    def copy(src, dst, send, recv, device):
        return Pieces(src, dst, send_sem.at[send], recv_sem.at[recv], device)

    def span(g, low, size):
        return held.at[pl.ds(starts[g], sizes[g]), :, pl.ds(low, size)]

    def edge(g, side, device):
        src = x.at[pl.ds(starts[g] % per_dev, sizes[g]), :, pl.ds(sides[side], HR)]
        return copy(src, span(g, sides[side], HR), 2 * g + side, 2 * g + side, device)

    def middle(p, device):
        src = x.at[p % per_dev, :, pl.ds(HR, rows - 2 * HR)]
        dst = held.at[p, :, pl.ds(HR, rows - 2 * HR)]
        at = mid_slot + p - per_dev
        return copy(src, dst, at, at, device)

    def onward_edge(side):
        low = sides[side]
        return copy(span(2, low, HR), span(0, low, HR), onward_slot + side, side, next_dev)

    def onward_middle(k):
        src = held.at[2 * per_dev + k, :, pl.ds(HR, rows - 2 * HR)]
        dst = held.at[per_dev + k, :, pl.ds(HR, rows - 2 * HR)]
        return copy(src, dst, onward_slot + 2 + k, mid_slot + k, next_dev)

    def onward_halo(side):
        low = rows + side * HR
        recv = (down_slot, up_slot)[side]
        send = onward_slot + 2 + far + side
        return copy(span(2, low, HR), span(0, low, HR), send, recv, next_dev)

    def down(g):
        return copy(span(g, rows - HR, HR), span(g, rows, HR), down_slot + g, down_slot + g, down_dev)

    def up(g):
        return copy(span(g, 0, HR), span(g, rows + HR, HR), up_slot + g, up_slot + g, up_dev)

    def own_down():
        src = x.at[:, :, pl.ds(rows - HR, HR)]
        dst = held.at[pl.ds(0, per_dev), :, pl.ds(rows, HR)]
        return copy(src, dst, own_slot, own_slot, down_dev)

    def own_up():
        src = x.at[:, :, pl.ds(0, HR)]
        dst = held.at[pl.ds(0, per_dev), :, pl.ds(rows + HR, HR)]
        return copy(src, dst, own_slot + 1, own_slot + 1, up_dev)

    has = [tm + 1 < tm_count, tm + 1 < tm_count, tm + 2 < tm_count]
    passes = even & has[2]
    sends = [odd, tm >= 1, tm >= 2]
    to = [near_dev, near_dev, far_dev]

    line_even = lax.rem(line, 2) == 0
    far_down, far_up = below & ~line_even, above & line_even
    goes_down = [below & (even | line_even), below, below]
    goes_up = [above & (even | ~line_even), above, above]

    def when(condition, action):
        @pl.when(condition)
        def _():
            action()

    def send_edges(g):
        for side in range(2):
            edge(g, side, to[g]).start()

    def send_middles(g):
        for k in range(sizes[g]):
            middle(starts[g] + k, to[g]).start()

    when(above, lambda: own_up().start())
    when(sends[2], lambda: send_edges(2))
    when(sends[0], lambda: send_edges(0))
    when(odd, lambda: send_edges(1))
    for local_copy in local_copies:
        local_copy.start()

    def relay(g):
        def act():
            for side in range(2):
                edge(g, side, to[g]).wait_recv()
            when(goes_down[g], lambda: down(g).start())
            when(goes_up[g], lambda: up(g).start())

        when(has[g], act)

    def halo(g):
        when(has[g] & below, lambda: up(g).wait_recv())
        when(has[g] & above, lambda: down(g).wait_recv())

    work = Slots(
        tm, line, acq_total, (per_dev, rows, cols), planes, power_sums, sums, lhs, bands, own_box,
        counts, looks,
    )
    inside = work.inside

    def lane(a, p):
        return a, p, planes.at[p], power.at[p], ifg.at[a, p - a - 1], coh.at[a, p - a - 1]

    def place(p, first, count, keep):
        work.place(held.at[p], planes.at[p], first, count, keep)

    for local_copy in local_copies:
        local_copy.wait()

    inner = lax.broadcasted_iota(jnp.int32, (3 * LANES, 2 * LANES), 0)
    across = lax.broadcasted_iota(jnp.int32, (3 * LANES, 2 * LANES), 1)
    source = jnp.where(inner < 2 * LANES + LANES // 2, inner, inner - 3 * LANES)
    distance = jnp.abs(source - across)

    @pl.loop(0, per_dev)
    def _(a):
        bands[a] = jnp.where(distance <= looks[1, a], 1.0, 0.0).astype(jnp.bfloat16)
        late = jnp.where(odd, last_partners(per_dev)[1], last_partners(per_dev)[0])
        factors[a, 0] = jnp.full((rows, LANES), work.outer(a), jnp.float32)
        for k in range(2):
            alive, scale = work.factors(a, late + k)
            factors[a, 1 + k] = jnp.full((rows, LANES), alive, jnp.float32)
            factors[a, 3 + k] = scale
        place(a, 0, rows, None)

    told(0, below)
    when(below, lambda: own_down().start())
    told(1, even & (tm + 1 < tm_count))
    told(2, even & (tm + 2 < tm_count))
    tell(3, even & (tm + 2 < tm_count), {"tm": tm + 2})
    told(3, even & (tm >= 2))
    when(even & sends[1], lambda: send_edges(1))
    when(sends[2], lambda: send_middles(2))
    when(sends[0], lambda: send_middles(0))
    when(odd, lambda: send_middles(1))

    own_pairs = [(a, p) for p in range(1, per_dev) for a in range(p)]

    def own_halo():
        when(above, lambda: own_down().wait_recv())
        when(below, lambda: own_up().wait_recv())

    def own_work():
        @pl.loop(0, per_dev)
        def _(a):
            place(a, rows, 2 * HR, inside)
            work.partner_power(planes.at[a], power.at[a])
            box = work.boxed_power(a, power.at[a])
            for m in range(half):
                own_box[a, m] = box[m]

        work.slots([lane(a, p) for a, p in own_pairs])
        work.step(None)

    outer_line = (line == 0) | (line == line_count - 1)

    @pl.when(outer_line)
    def _():
        own_halo()
        own_work()

    relay(2)

    @pl.when(passes)
    def _():
        for side in range(2):
            onward_edge(side).start()

    when(even, lambda: relay(0))
    when(~outer_line, own_halo)
    when(even & sends[1], lambda: send_middles(1))
    when(odd, lambda: relay(1))
    when(~outer_line, own_work)
    when(even, lambda: relay(1))

    @pl.when(has[2])
    def _():
        for k in range(far):
            middle(2 * per_dev + k, far_dev).wait_recv()
            when(passes, lambda: onward_middle(k).start())

    def partners(chosen, there, placed=False):
        def prologue():
            for p, _ in chosen:
                if not placed:
                    place(p, 0, rows, there)
                place(p, rows, 2 * HR, inside & there)
            for p, _ in chosen:
                work.partner_power(planes.at[p], power.at[p])

        chosen_lanes = [lane(a, p) for p, first in chosen for a in range(first, per_dev)]
        work.slots(chosen_lanes, prologue)

    ends = [2 * per_dev + k for k in range(far)]
    for p in ends:
        place(p, 0, rows, has[2])
    halo(2)
    when(passes & far_up, lambda: onward_halo(0).start())
    when(passes & far_down, lambda: onward_halo(1).start())
    partners([(p, p - MAXP) for p in ends], has[2], placed=True)
    when(odd, lambda: relay(0))

    def arrived(p):
        g = 0 if p < starts[1] else 1
        when(has[g], lambda: middle(p, to[g]).wait_recv())
        if p == starts[g]:
            halo(g)

    def arrive(group):
        for p in group:
            arrived(p)

    turns, swapped = turn_order(per_dev)
    for n in range(0, per_dev, 2):
        when(even, lambda: arrive(turns[n : n + 2]))
        when(odd, lambda: arrive(swapped[n : n + 2]))
        both = zip(turns[n : n + 2], swapped[n : n + 2])
        if n + 2 < per_dev:
            partners([(jnp.where(odd, p_odd, p_even), 0) for p_even, p_odd in both], has[0])
    work.step(None)

    when(above, lambda: own_up().wait_send())
    when(below, lambda: own_down().wait_send())
    for g in range(3):
        when(has[g] & goes_down[g], lambda: down(g).wait_send())
        when(has[g] & goes_up[g], lambda: up(g).wait_send())

        @pl.when(sends[g])
        def _():
            for side in range(2):
                edge(g, side, to[g]).wait_send()
            for k in range(sizes[g]):
                middle(starts[g] + k, to[g]).wait_send()

    @pl.when(passes)
    def _():
        for side in range(2):
            onward_edge(side).wait_send()
        for k in range(far):
            onward_middle(k).wait_send()
        when(far_up, lambda: onward_halo(0).wait_send())
        when(far_down, lambda: onward_halo(1).wait_send())


def computed(x, counts, looks, acq_total):
    per_dev, parts, rows, cols = x.shape
    total, ext_rows = per_dev + MAXP, rows + 2 * HR
    tiles = cols // LANES
    slots = 16 + 2 * MAXP
    spare = max(0, 2 * per_dev - 1 - MAXP)
    hbm, vmem = [pl.BlockSpec(memory_space=space) for space in (pltpu.HBM, pltpu.VMEM)]
    return pl.pallas_call(
        functools.partial(kernel, acq_total),
        in_specs=[hbm, hbm, hbm],
        out_specs=[vmem] * 7,
        out_shape=[
            jax.ShapeDtypeStruct((per_dev, MAXP + spare, 2, rows, cols), jnp.bfloat16),
            jax.ShapeDtypeStruct((per_dev, MAXP + spare, rows, cols), jnp.bfloat16),
            jax.ShapeDtypeStruct((total, parts, 2 * rows, cols), x.dtype),
            jax.ShapeDtypeStruct((total, parts, ext_rows * tiles, LANES), jnp.float32),
            jax.ShapeDtypeStruct((per_dev, 3 * LANES, 2 * LANES), jnp.bfloat16),
            jax.ShapeDtypeStruct((per_dev, tiles // 2, rows, 2 * LANES), jnp.float32),
            jax.ShapeDtypeStruct((per_dev, 5, rows, LANES), jnp.float32),
        ],
        scratch_shapes=[
            pltpu.VMEM((total, 2, tiles // 2 * rows, 3 * LANES), jnp.bfloat16),
            pltpu.VMEM((2, tiles * rows, LANES), jnp.float32),
            pltpu.VMEM((2, tiles * rows, LANES), jnp.float32),
            pltpu.VMEM((tiles * rows, 3 * LANES), jnp.bfloat16),
            pltpu.SMEM((per_dev,), jnp.int32),
            pltpu.SMEM((2, per_dev), jnp.int32),
            pltpu.SemaphoreType.DMA((slots,)),
            pltpu.SemaphoreType.DMA((slots,)),
            pltpu.SemaphoreType.DMA((3,)),
            pltpu.SemaphoreType.REGULAR((4,)),
        ],
        compiler_params=pltpu.CompilerParams(
            collective_id=0, has_side_effects=True, vmem_limit_bytes=40 * 1024 * 1024
        ),
        name="insar_boxes",
    )(*[pltpu.with_memory_space_constraint(operand, pltpu.HBM) for operand in (counts, looks, x)])


def write(
    acq_total, ifg, coh, held, planes, bands, own_box, factors, ifg_out, coh_out,
    late_ifg, late_coh, late_planes, power, power_sums, sums, lhs, sem,
):
    tm, line = lax.axis_index("tm"), lax.axis_index("rows")
    per_dev, _, _, rows, cols = ifg.shape
    even, odd = lax.rem(tm, 2) == 0, lax.rem(tm, 2) == 1
    starts = last_partners(per_dev)

    def copies(start, a, late):
        low, high = start - a - 1, min(start - a + 1, MAXP)
        found = []
        for n, (src, kept, dst) in enumerate(((ifg, late_ifg, ifg_out), (coh, late_coh, coh_out))):
            slot = 6 * a + 3 * n
            if late:
                piece = kept.at[a, pl.ds(0, high - low)]
                found.append((piece, dst.at[a, pl.ds(low, high - low)], slot))
                continue
            for k, (first, end) in enumerate(((0, low), (high, MAXP))):
                if first < end:
                    span = pl.ds(first, end - first)
                    found.append((src.at[a, span], dst.at[a, span], slot + 1 + k))
        return [pltpu.make_async_copy(src, dst, sem.at[slot]) for src, dst, slot in found]

    def each(act, late, which):
        for there, start in zip((even, odd), starts):

            @pl.when(there)
            def _():
                for a in which:
                    for copy in copies(start, a, late):
                        act(copy)

    each(lambda copy: copy.start(), False, range(per_dev))
    work = LateSlots(
        tm, line, acq_total, (per_dev, rows, cols), planes, power_sums, sums, lhs, bands, own_box,
        factors, None,
    )
    there = tm + 1 < lax.axis_size("tm")
    first = jnp.where(odd, starts[1], starts[0])
    for k in range(2):
        work.place(held.at[first + k], late_planes.at[k], 0, rows, there)
        work.place(held.at[first + k], late_planes.at[k], rows, 2 * HR, work.inside & there)
        work.partner_power(late_planes.at[k], power.at[k])
    for a in range(per_dev):
        for k in range(2):
            work.step(
                (a, k, late_planes.at[k], power.at[k], late_ifg.at[a, k], late_coh.at[a, k])
            )
            if a > 0 and k == 0:
                each(lambda copy: copy.start(), True, [a - 1])
    work.step(None)
    each(lambda copy: copy.start(), True, [per_dev - 1])
    each(lambda copy: copy.wait(), False, range(per_dev))
    each(lambda copy: copy.wait(), True, range(per_dev))


def turn_order(per_dev):
    far = MAXP - per_dev
    turns = list(range(per_dev, 2 * per_dev))
    return turns, turns[far:] + turns[:far]


def last_partners(per_dev):
    turns, swapped = turn_order(per_dev)
    return turns[-2], swapped[-2]


def written(acq_total, ifg, coh, held, planes, bands, own_box, factors):
    per_dev, _, _, rows, cols = ifg.shape
    tiles, ext_rows = cols // LANES, rows + 2 * HR
    hbm, vmem = [pl.BlockSpec(memory_space=space) for space in (pltpu.HBM, pltpu.VMEM)]
    return pl.pallas_call(
        functools.partial(write, acq_total),
        in_specs=[vmem] * 7,
        out_specs=[hbm, hbm],
        out_shape=[
            jax.ShapeDtypeStruct((per_dev, MAXP, 2, rows, cols), jnp.bfloat16),
            jax.ShapeDtypeStruct((per_dev, MAXP, rows, cols), jnp.bfloat16),
        ],
        scratch_shapes=[
            pltpu.VMEM((per_dev, 2, 2, rows, cols), jnp.bfloat16),
            pltpu.VMEM((per_dev, 2, rows, cols), jnp.bfloat16),
            pltpu.VMEM((2, 2, ext_rows * tiles, LANES), jnp.float32),
            pltpu.VMEM((2, 2, tiles // 2 * rows, 3 * LANES), jnp.bfloat16),
            pltpu.VMEM((2, tiles * rows, LANES), jnp.float32),
            pltpu.VMEM((2, tiles * rows, LANES), jnp.float32),
            pltpu.VMEM((tiles * rows, 3 * LANES), jnp.bfloat16),
            pltpu.SemaphoreType.DMA((6 * per_dev,)),
        ],
        compiler_params=pltpu.CompilerParams(vmem_limit_bytes=12 * 1024 * 1024),
        name="insar_write",
    )(ifg, coh, held, planes, bands, own_box, factors)


def local(slc_stack, partner_count, look_sizes):
    acq_total = lax.axis_size("tm") * slc_stack.shape[0]
    looks = look_sizes.T
    found = computed(slc_stack, partner_count, looks, acq_total)
    return tuple(written(acq_total, *found))


def solution(mesh):
    return jax.shard_map(
        local,
        mesh=mesh,
        in_specs=(P("tm", None, "rows", None), P("tm"), P("tm", None)),
        out_specs=(P("tm", None, None, "rows", None), P("tm", None, "rows", None)),
        check_vma=False,
    )
```
